32 devices in a mesh: grp: 2 (over x), seq: 16 (over z, y, core).
Axes of the slice: x: 2, y: 2, z: 4, core: 2. Of those that a mesh axis runs over, the one named last changes fastest.
Arguments:
- queries: bfloat16 [4096, 8192], P(('grp', 'seq')), parts along dimension 0, may hold values from -8 to 8, as said below
- new_kv: bfloat16 [4096, 2048], P(('grp', 'seq')), parts along dimension 0, may hold values from -6 to 6
- cache: bfloat16 [32, 8192, 256], P(('grp', 'seq')), parts along dimension 0, may hold values from -4 to 4, as said below
- tile_lists: int32 [128, 16, 8], P(('grp', 'seq')), parts along dimension 0, may hold values from 0 to 63, as said below
- tile_counts: int32 [128, 16], P(('grp', 'seq')), parts along dimension 0, may hold values from 1 to 8, as said below
- tile_mask: int32 [32, 16], P('grp'), parts along dimension 0, may hold values from 0 to 1, as said below
Outputs:
- attended: bfloat16 [4096, 8192], P(('grp', 'seq')), parts along dimension 0
The draws below stay inside these ranges and needn't reach their ends.
There are 2 independent parts, one for each index of `grp`. The reference program is written for one: setup_inputs(seed, part) draws one part's arguments, and reference() takes and returns one part's arrays. A program takes and returns all parts, laid end to end along the dimension named above; each array names one. Nothing has to cross between parts.
Inputs may be any that keep to these rules, and one draw needn't show every extreme that they name: `queries`: row t, query head h: positions and heads laid out as stated; values within the range. cache[d] is the cache of kv head d * 8 // 16; the 2 copies of one kv head are equal. `tile_lists`: the valid slots of a list name different cache tiles; slots past the count hold tile numbers that are not attended. `tile_counts`: some list of some head has all 8 slots valid. `tile_mask`: the diagonal is 1, every entry above it is 0, and entry (i, j) is 0 wherever j // 4 < i // 4 - 3.
All inputs are finite; a program needn't handle non-finite values.
Results may differ from the reference program's by a relative error of at most 0.0065.
Values may be sent and summed in bfloat16 or wider, within the bound.
A program may use at most 128 MiB of HBM per device.

```python
import math
import jax
import jax.numpy as jnp
from jax import lax

H = 64
KVH = 8
HD = 128
TILE = 128
LIST = 8
REACH = 3
CTX = 8192
TOKENS = 2048
OWNERS = 16
QT = 16
CT = 64


def draw_queries(key, part):
    base = jnp.clip(jax.random.normal(jax.random.fold_in(key, 17), (TOKENS, H, HD), jnp.float32), -6.0, 6.0)
    return base.reshape(TOKENS, H * HD).astype(jnp.bfloat16)


def draw_cache(key, part):
    per_group = jnp.clip(jax.random.normal(jax.random.fold_in(key, 23), (KVH, CTX, 2 * HD), jnp.float32), -4.0, 4.0)
    return jnp.repeat(per_group, OWNERS // KVH, axis=0).astype(jnp.bfloat16)


def draw_tile_lists(key, part):
    split_keys = jax.random.split(jax.random.fold_in(key, 31), H * QT)
    orders = jax.vmap(lambda one_key: jax.random.permutation(one_key, CT))(split_keys)
    return orders[:, :LIST].reshape(H, QT, LIST).astype(jnp.int32)


def draw_tile_counts(key, part):
    shifts = jax.random.randint(jax.random.fold_in(key, 37), (H,), 0, 3)
    full_head = jax.random.randint(jax.random.fold_in(key, 41), (), 0, H)
    shifts = jnp.where(jnp.arange(H) == full_head, 0, shifts)
    ceiling = jnp.maximum(LIST // jnp.left_shift(jnp.int32(1), shifts), 1)
    counts = jax.random.randint(jax.random.fold_in(key, 43), (H, QT), 1, ceiling[:, None] + 1)
    peak_tile = jax.random.randint(jax.random.fold_in(key, 47), (H,), 0, QT)
    counts = jnp.where(jnp.arange(QT)[None, :] == peak_tile[:, None], ceiling[:, None], counts)
    return counts.astype(jnp.int32)


def draw_tile_mask(key, part):
    coin = jax.random.randint(jax.random.fold_in(key, 53), (QT, QT), 0, 4)
    row_ids = jnp.arange(QT)[:, None]
    col_ids = jnp.arange(QT)[None, :]
    within_reach = col_ids // 4 >= row_ids // 4 - REACH
    below = (col_ids < row_ids) & (coin > 0) & within_reach
    return jnp.where((col_ids == row_ids) | below, 1, 0).astype(jnp.int32)


def shard_levels(stream_key, shape, shards, low, high):
    loudness, own = 1.0, jax.random.fold_in(stream_key, 6)
    for axis_at, parts in shards:
        steps = jnp.exp(jax.random.uniform(jax.random.fold_in(own, axis_at), (parts,), jnp.float32, low / len(shards), high / len(shards)))
        loudness = loudness * jnp.repeat(steps, shape[axis_at] // parts).reshape([-1 if axis == axis_at else 1 for axis in range(len(shape))])
    return loudness


def scatter_about(own_key, shape, deviation, bound, pieces=(), kind=jnp.bfloat16):
    values = deviation * jax.random.normal(own_key, shape, jnp.float32)
    if pieces:
        values = values * shard_levels(own_key, shape, pieces, -0.22, 0.18)
    return jnp.clip(values, -bound, bound).astype(kind)


def setup_inputs(seed: int = 0, part: int = 0) -> dict:
    arg_keys = jax.random.split(jax.random.key(seed), 7)
    part_keys = jax.random.split(jax.random.fold_in(arg_keys[6], part), 7)
    return {
        "queries": draw_queries(jax.random.fold_in(jax.random.fold_in(arg_keys[6], part), 71), part),
        "new_kv": scatter_about(part_keys[1], (TOKENS, 2 * KVH * HD), 1.0, 6.0, ((0, 16),)),
        "cache": draw_cache(jax.random.fold_in(jax.random.fold_in(arg_keys[6], part), 71), part),
        "tile_lists": draw_tile_lists(jax.random.fold_in(jax.random.fold_in(arg_keys[6], part), 71), part),
        "tile_counts": draw_tile_counts(jax.random.fold_in(jax.random.fold_in(arg_keys[6], part), 71), part),
        "tile_mask": draw_tile_mask(jax.random.fold_in(jax.random.fold_in(arg_keys[6], part), 71), part),
    }


def reference(queries, new_kv, cache, tile_lists, tile_counts, tile_mask):
    tokens = queries.shape[0]
    factor = 1.0 / math.sqrt(HD)
    positions = jnp.arange(tokens)
    tile_of = positions // TILE
    span_allowed = (tile_mask[tile_of][:, tile_of] > 0) & (positions[None, :] <= positions[:, None])
    heads_owner = H // OWNERS
    heads_group = H // KVH

    def one_head(head_num):
        q_head = lax.dynamic_slice_in_dim(queries, head_num * HD, HD, 1)
        group_num = head_num // heads_group
        kv_part = lax.dynamic_slice_in_dim(new_kv, group_num * 2 * HD, 2 * HD, 1)
        span_keys = kv_part[:, :HD]
        span_values = kv_part[:, HD:]
        owner_cache = lax.dynamic_index_in_dim(cache, head_num // heads_owner, 0, keepdims=False)
        cache_keys = owner_cache[:, :HD].reshape(CT, TILE, HD)
        cache_values = owner_cache[:, HD:].reshape(CT, TILE, HD)
        picked = lax.dynamic_index_in_dim(tile_lists, head_num, 0, keepdims=False)
        counts_here = lax.dynamic_index_in_dim(tile_counts, head_num, 0, keepdims=False)
        listed_keys = cache_keys[picked].reshape(QT, LIST * TILE, HD).astype(jnp.float32)
        listed_values = cache_values[picked].reshape(QT, LIST * TILE, HD).astype(jnp.float32)
        live = jnp.repeat(jnp.arange(LIST)[None, :] < counts_here[:, None], TILE, axis=1)
        q_tiles = q_head.reshape(QT, TILE, HD).astype(jnp.float32)
        cache_scores = jnp.einsum('atd,akd->atk', q_tiles, listed_keys) * factor
        cache_scores = jnp.where(live[:, None, :], cache_scores, -jnp.inf)
        span_scores = jnp.dot(q_head, span_keys.T, preferred_element_type=jnp.float32) * factor
        span_scores = jnp.where(span_allowed, span_scores, -jnp.inf)
        peak = jnp.maximum(lax.optimization_barrier(jnp.max(cache_scores.reshape(tokens, LIST * TILE), axis=1)), lax.optimization_barrier(jnp.max(span_scores, axis=1)))
        cache_weights = jnp.exp(cache_scores - peak.reshape(QT, TILE)[:, :, None])
        span_weights = jnp.exp(span_scores - peak[:, None])
        total = lax.optimization_barrier(jnp.sum(cache_weights.reshape(tokens, LIST * TILE), axis=1)) + lax.optimization_barrier(jnp.sum(span_weights, axis=1))
        cache_bf = cache_weights.astype(jnp.bfloat16).astype(jnp.float32)
        span_bf = span_weights.astype(jnp.bfloat16)
        cache_mix = jnp.einsum('atk,akd->atd', cache_bf, listed_values).reshape(tokens, HD)
        span_mix = jnp.dot(span_bf, span_values, preferred_element_type=jnp.float32)
        return ((cache_mix + span_mix) / total[:, None]).astype(jnp.bfloat16)
    outputs = lax.map(one_head, jnp.arange(H))
    return outputs.transpose(1, 0, 2).reshape(tokens, H * HD)
```

```python
import functools
import math

import jax
import jax.numpy as jnp
from jax import lax
from jax.experimental import pallas as pl
from jax.experimental.pallas import tpu as pltpu
from jax.sharding import PartitionSpec as P

TILE = 128
REACH = 3
GROUP = 4
MESH = pl.DeviceIdType.MESH
NEG = -jnp.inf


def dot_t(a, b):
    return lax.dot_general(a, b, (((1,), (1,)), ((), ())), preferred_element_type=jnp.float32)


def keep_if(value, above, part):
    return jnp.where(jnp.full(part.shape, value, jnp.int32) > above, part, NEG)


def attend_block(h, b, slots, qbuf, kvbuf, cbuf, lists, counts, mask, scores, peaks, accum, obuf):
    hd = qbuf.shape[-1]
    rows = GROUP * TILE
    scale = math.log2(math.e) / math.sqrt(hd)
    base = pl.multiple_of(b * rows, rows)
    first = jnp.maximum(b - REACH, 0)
    span_at = slots * TILE

    def cache_scores(t, _):
        tile = b * GROUP + t
        count = counts[h, tile]
        start = pl.multiple_of(base + t * TILE, TILE)
        here = pl.ds(pl.multiple_of(t * TILE, TILE), TILE)
        q = qbuf[h, pl.ds(start, TILE), :]
        top = None
        for j in range(0, slots, 2):
            keys = jnp.concatenate(
                [cbuf[lists[h, j + k, tile], :, :hd] for k in range(2)], axis=0
            )
            s = dot_t(q, keys)
            for k in range(2):
                part = keep_if(count, j + k, s[:, k * TILE : (k + 1) * TILE])
                scores[here, (j + k) * TILE : (j + k + 1) * TILE] = part
                top = part if top is None else jnp.maximum(top, part)
        peaks[here, :] = top
        return 0

    lax.fori_loop(0, GROUP, cache_scores, 0, unroll=True)

    def span_scores(kb, diagonal):
        q = qbuf[h, pl.ds(base, rows), :]
        col = pl.multiple_of(span_at + (kb - first) * rows, rows)
        if diagonal:
            lower = lax.broadcasted_iota(jnp.int32, (TILE, TILE), 1) <= lax.broadcasted_iota(
                jnp.int32, (TILE, TILE), 0
            )
        for half in range(2):
            keys = kvbuf[kb * 2 + half, :, :, :hd].reshape(2 * TILE, hd)
            s = dot_t(q, keys)
            for t in range(GROUP):
                top = peaks[t * TILE : (t + 1) * TILE, :]
                for k in range(2):
                    u = half * 2 + k
                    part = s[t * TILE : (t + 1) * TILE, k * TILE : (k + 1) * TILE]
                    if diagonal and u > t:
                        part = jnp.full((TILE, TILE), NEG, jnp.float32)
                    else:
                        if diagonal and u == t:
                            part = jnp.where(lower, part, NEG)
                        part = keep_if(mask[b * GROUP + t, kb * GROUP + u], 0, part)
                        top = jnp.maximum(top, part)
                    scores[t * TILE : (t + 1) * TILE, pl.ds(col + u * TILE, TILE)] = part
                peaks[t * TILE : (t + 1) * TILE, :] = top

    def off_diagonal(kb, _):
        span_scores(kb, False)
        return 0

    lax.fori_loop(first, b, off_diagonal, 0)
    span_scores(b, True)

    def cache_mix(t, _):
        tile = b * GROUP + t
        here = pl.ds(pl.multiple_of(t * TILE, TILE), TILE)
        peak = jnp.max(peaks[here, :], axis=1, keepdims=True)
        peak = jnp.broadcast_to(peak, (TILE, TILE))
        peaks[here, :] = peak
        ones = jnp.ones((TILE, hd), jnp.bfloat16)
        total = None
        for j in range(0, slots, 2):
            values = jnp.concatenate(
                [
                    jnp.concatenate([cbuf[lists[h, j + k, tile], :, hd:], ones], axis=1)
                    for k in range(2)
                ],
                axis=0,
            )
            weights = jnp.concatenate(
                [
                    jnp.exp2(
                        (scores[here, (j + k) * TILE : (j + k + 1) * TILE] - peak) * scale
                    ).astype(jnp.bfloat16)
                    for k in range(2)
                ],
                axis=1,
            )
            mixed = jnp.dot(weights, values, preferred_element_type=jnp.float32)
            total = mixed if total is None else total + mixed
        accum[here, :] = total
        return 0

    lax.fori_loop(0, GROUP, cache_mix, 0, unroll=True)

    def span_mix(kb, _):
        col = pl.multiple_of(span_at + (kb - first) * rows, rows)
        ones = jnp.ones((rows, hd), jnp.bfloat16)
        values = kvbuf[pl.ds(kb * 2, 2), :, :, hd:].reshape(rows, hd)
        values = jnp.concatenate([values, ones], axis=1)
        for t in range(GROUP):
            here = slice(t * TILE, (t + 1) * TILE)
            peak = peaks[here, :]
            weights = jnp.concatenate(
                [
                    jnp.exp2(
                        (scores[here, pl.ds(col + u * TILE, TILE)] - peak) * scale
                    ).astype(jnp.bfloat16)
                    for u in range(GROUP)
                ],
                axis=1,
            )
            accum[here, :] += jnp.dot(weights, values, preferred_element_type=jnp.float32)
        return 0

    lax.fori_loop(first, b + 1, span_mix, 0)
    obuf[h, pl.ds(base, rows), :] = (accum[:, :hd] / accum[:, hd:]).astype(jnp.bfloat16)


def fused(
    n, kv_heads, slots,
    lists_ref, counts_ref, mask_ref, q_ref, kv_ref, c_ref, out_ref,
    lists, counts, mask, qbuf, kvbuf, cbuf, obuf, scores, peaks, accum,
    above_sem, below_sem, s_sem, c_sem, l_sem, kv_send, kv_recv, f_send, f_recv, q_send, q_recv, o_send, o_recv,
):
    me = lax.axis_index("seq")
    heads, _, hd = qbuf.shape
    chips = n // 2
    core = lax.rem(me, 2)
    sibling = me + 1 - 2 * core
    my_chip = me // 2

    blocks = n // GROUP
    half = blocks // 2

    def far_first(step):
        z = me // GROUP
        upper = z // half
        across = 1 - step // half
        far = lax.rem(step, half)
        near = lax.rem(z + 1 + step, half)
        low = jnp.where(across == 1, far, near)
        high = jnp.where(across == 1, half - 1 - far, near)
        target = lax.rem(upper + across, 2)
        return target * half + jnp.where(target == 0, low, high)

    levels = n // GROUP
    level = me // GROUP
    pos = lax.rem(me, GROUP)
    has_above = level + 1 < levels
    has_below = level > 0
    barrier = pltpu.get_barrier_semaphore()

    def tell(sem, device):
        pl.semaphore_signal(sem, inc=1, device_id={"seq": device}, device_id_type=MESH)

    for k in range(1, GROUP):
        tell(barrier, level * GROUP + lax.rem(pos + k, GROUP))

    @pl.when(has_above)
    def _():
        tell(barrier, me + GROUP)

    @pl.when(has_below)
    def _():
        tell(barrier, me - GROUP)

    cache_copy = pltpu.make_async_copy(c_ref, cbuf, c_sem)
    cache_copy.start()

    small = [
        pltpu.make_async_copy(src, dst, s_sem.at[k])
        for k, (src, dst) in enumerate(((lists_ref, lists), (counts_ref, counts), (mask_ref, mask)))
    ]
    for copy in small:
        copy.start()
    def own_q(h):
        return pltpu.make_async_copy(
            q_ref.at[:, pl.ds(pl.multiple_of((me * heads + h) * hd, hd), hd)],
            qbuf.at[h, pl.ds(pl.multiple_of(me * TILE, TILE), TILE), :],
            l_sem.at[h],
        )

    def kv_cols(chip):
        return pl.ds(pl.multiple_of((2 * chip * kv_heads // n) * 2 * hd, 2 * hd), 2 * hd)

    own_kv = pltpu.make_async_copy(kv_ref.at[:, kv_cols(my_chip)], kvbuf.at[my_chip, core], l_sem.at[heads])
    own_kv.start()
    for h in range(heads):
        own_q(h).start()
    pl.semaphore_wait(barrier, GROUP - 1 + has_above.astype(jnp.int32) + has_below.astype(jnp.int32))

    def send_kv(chip):
        pltpu.make_async_remote_copy(
            src_ref=kv_ref.at[:, kv_cols(chip)],
            dst_ref=kvbuf.at[my_chip, core],
            send_sem=kv_send,
            recv_sem=kv_recv,
            device_id={"seq": 2 * chip + core},
            device_id_type=MESH,
        ).start()

    pairs = GROUP // 2

    def kv_to_level(at, first):
        for k in range(first, pairs):
            send_kv(at * pairs + lax.rem(pos // 2 + k, pairs))

    @pl.when(has_above)
    def _():
        tell(below_sem, me + GROUP)
        send_kv(my_chip + pairs)

    @pl.when(has_below)
    def _():
        tell(above_sem, me - GROUP)
        send_kv(my_chip - pairs)

    def learn(k, first):
        @pl.when(level + k < levels)
        def _():
            pl.semaphore_wait(above_sem, 1)

            @pl.when(has_below)
            def _():
                tell(above_sem, me - GROUP)

            kv_to_level(level + k, first)

        @pl.when(level >= k)
        def _():
            pl.semaphore_wait(below_sem, 1)

            @pl.when(has_above)
            def _():
                tell(below_sem, me + GROUP)

            kv_to_level(level - k, first)

        return 0

    learn(1, 1)
    lax.fori_loop(2, levels, lambda k, _: learn(k, 0), 0)
    kv_to_level(level, 1)

    def send_q(step, _):
        h = step // n
        turn = lax.rem(step, n)
        peer = far_first(turn // GROUP) * GROUP + lax.rem(me + turn, GROUP)

        @pl.when(peer != me)
        def _():
            pltpu.make_async_remote_copy(
                src_ref=q_ref.at[:, pl.ds(pl.multiple_of((peer * heads + h) * hd, hd), hd)],
                dst_ref=qbuf.at[h, pl.ds(pl.multiple_of(me * TILE, TILE), TILE), :],
                send_sem=q_send,
                recv_sem=q_recv.at[h],
                device_id={"seq": peer},
                device_id_type=MESH,
            ).start()

        return 0

    lax.fori_loop(0, heads * n, send_q, 0)

    def take(ref, sem):
        pltpu.make_async_copy(ref, ref, sem).wait()

    own_kv.wait()
    take(kvbuf.at[pl.ds(0, chips - 1), 0], kv_recv)
    forward = pltpu.make_async_remote_copy(
        src_ref=kvbuf.at[:, core],
        dst_ref=kvbuf.at[:, core],
        send_sem=f_send,
        recv_sem=f_recv,
        device_id={"seq": sibling},
        device_id_type=MESH,
    )
    forward.start()
    cache_copy.wait()
    for copy in small:
        copy.wait()
    forward.wait()

    def one_head(h, _):
        own_q(h).wait()
        take(qbuf.at[h, pl.ds(0, (n - 1) * TILE), :], q_recv.at[h])

        def one_block(step, _):
            b = far_first(step)
            attend_block(
                h, b, slots, qbuf, kvbuf, cbuf, lists, counts, mask, scores, peaks, accum, obuf
            )
            cols = pl.ds(pl.multiple_of((me * heads + h) * hd, hd), hd)
            for t in range(GROUP):
                peer = b * GROUP + t
                src = obuf.at[h, pl.ds(pl.multiple_of(peer * TILE, TILE), TILE), :]

                @pl.when(peer != me)
                def _():
                    pltpu.make_async_remote_copy(
                        src_ref=src,
                        dst_ref=out_ref.at[:, cols],
                        send_sem=o_send,
                        recv_sem=o_recv,
                        device_id={"seq": peer},
                        device_id_type=MESH,
                    ).start()

                @pl.when(peer == me)
                def _():
                    pltpu.make_async_copy(src, out_ref.at[:, cols], l_sem.at[heads + 1]).start()

            return 0

        lax.fori_loop(0, blocks, one_block, 0)
        return 0

    lax.fori_loop(0, heads, one_head, 0)

    wide = pl.ds(0, (n - 1) * heads * hd)
    take(kvbuf.at[pl.ds(0, chips - 1), 0], kv_send)
    take(q_ref.at[:, wide], q_send)
    take(q_ref.at[:, wide], o_send)
    take(out_ref.at[:, wide], o_recv)
    take(out_ref.at[:, pl.ds(0, heads * hd)], l_sem.at[heads + 1])


def per_device(queries, new_kv, cache, tile_lists, tile_counts, tile_mask):
    n = lax.axis_size("seq")
    hd = cache.shape[2] // 2
    kv_heads = new_kv.shape[1] // (2 * hd)
    heads, tiles, slots = tile_lists.shape
    tokens = tiles * TILE
    rows = GROUP * TILE
    reach = min(REACH + 1, tiles // GROUP)
    bf, f32 = jnp.bfloat16, jnp.float32
    dma = pltpu.SemaphoreType.DMA
    hbm = pl.BlockSpec(memory_space=pl.ANY)
    return pl.pallas_call(
        functools.partial(fused, n, kv_heads, slots),
        out_shape=pltpu.VMEM(queries.shape, bf),
        in_specs=[hbm] * 6,
        out_specs=hbm,
        scratch_shapes=[
            pltpu.SMEM((heads, slots, tiles), jnp.int32),
            pltpu.SMEM((heads, tiles), jnp.int32),
            pltpu.SMEM(tile_mask.shape, jnp.int32),
            pltpu.VMEM((heads, tokens, hd), bf),
            pltpu.VMEM((n // 2, 2, TILE, 2 * hd), bf),
            pltpu.VMEM((cache.shape[1] // TILE, TILE, 2 * hd), bf),
            pltpu.VMEM((heads, tokens, hd), bf),
            pltpu.VMEM((rows, slots * TILE + reach * rows), f32),
            pltpu.VMEM((rows, TILE), f32),
            pltpu.VMEM((rows, 2 * hd), f32),
            pltpu.SemaphoreType.REGULAR, pltpu.SemaphoreType.REGULAR,
            dma((3,)), dma, dma((heads + 2,)), dma, dma, dma, dma, dma, dma((heads,)), dma, dma,
        ],
        compiler_params=pltpu.CompilerParams(
            collective_id=0, has_side_effects=True, vmem_limit_bytes=60 * 1024 * 1024
        ),
    )(tile_lists.transpose(0, 2, 1), tile_counts, tile_mask, queries, new_kv, cache.reshape(-1, TILE, 2 * hd))


def solution(mesh):
    placed = (
        P(("grp", "seq"), None),
        P(("grp", "seq"), None),
        P(("grp", "seq"), None, None),
        P(("grp", "seq"), None, None),
        P(("grp", "seq"), None),
        P("grp", None),
    )
    return jax.shard_map(
        per_device, mesh=mesh, in_specs=placed, out_specs=P(("grp", "seq"), None), check_vma=False
    )
```

```python
import functools
import math

import jax
import jax.numpy as jnp
from jax import lax
from jax.experimental import pallas as pl
from jax.experimental.pallas import tpu as pltpu
from jax.sharding import PartitionSpec as P

TILE = 128
REACH = 3
GROUP = 4
MESH = pl.DeviceIdType.MESH
NEG = -jnp.inf


def dot_t(a, b):
    return lax.dot_general(a, b, (((1,), (1,)), ((), ())), preferred_element_type=jnp.float32)


def keep_if(value, above, part):
    return jnp.where(jnp.full(part.shape, value, jnp.int32) > above, part, NEG)


def attend_block(
    h, b, slots, qbuf, kvbuf, cbuf, lists, counts, mask, scores, peaks, accum, obuf, stats=None, half=0
):
    hd = qbuf.shape[-1]
    rows = GROUP * TILE
    scale = math.log2(math.e) / math.sqrt(hd)
    base = pl.multiple_of(b * rows, rows)
    first = jnp.maximum(b - REACH, 0)
    span_at = slots * TILE

    def cache_scores(t, _):
        tile = b * GROUP + t
        count = counts[h, tile]
        start = pl.multiple_of(base + t * TILE, TILE)
        here = pl.ds(pl.multiple_of(t * TILE, TILE), TILE)
        q = qbuf[h, pl.ds(start, TILE), :]
        top = None
        for j in range(0, slots, 2):
            keys = jnp.concatenate(
                [cbuf[lists[h, j + k, tile], :, :hd] for k in range(2)], axis=0
            )
            s = dot_t(q, keys)
            for k in range(2):
                part = keep_if(count, j + k, s[:, k * TILE : (k + 1) * TILE])
                scores[here, (j + k) * TILE : (j + k + 1) * TILE] = part
                top = part if top is None else jnp.maximum(top, part)
        peaks[here, :] = top
        return 0

    lax.fori_loop(0, GROUP, cache_scores, 0, unroll=True)

    def span_scores(kb, diagonal):
        q = qbuf[h, pl.ds(base, rows), :]
        col = pl.multiple_of(span_at + (kb - first) * rows, rows)
        if diagonal:
            lower = lax.broadcasted_iota(jnp.int32, (TILE, TILE), 1) <= lax.broadcasted_iota(
                jnp.int32, (TILE, TILE), 0
            )
        for half in range(2):
            keys = kvbuf[kb * 2 + half, :, :, :hd].reshape(2 * TILE, hd)
            s = dot_t(q, keys)
            for t in range(GROUP):
                top = peaks[t * TILE : (t + 1) * TILE, :]
                for k in range(2):
                    u = half * 2 + k
                    part = s[t * TILE : (t + 1) * TILE, k * TILE : (k + 1) * TILE]
                    if diagonal and u > t:
                        part = jnp.full((TILE, TILE), NEG, jnp.float32)
                    else:
                        if diagonal and u == t:
                            part = jnp.where(lower, part, NEG)
                        part = keep_if(mask[b * GROUP + t, kb * GROUP + u], 0, part)
                        top = jnp.maximum(top, part)
                    scores[t * TILE : (t + 1) * TILE, pl.ds(col + u * TILE, TILE)] = part
                peaks[t * TILE : (t + 1) * TILE, :] = top

    def off_diagonal(kb, _):
        span_scores(kb, False)
        return 0

    lax.fori_loop(first, b if stats is None else half // GROUP, off_diagonal, 0)
    if stats is None:
        span_scores(b, True)

    def cache_mix(t, _):
        tile = b * GROUP + t
        here = pl.ds(pl.multiple_of(t * TILE, TILE), TILE)
        peak = jnp.max(peaks[here, :], axis=1, keepdims=True)
        peak = jnp.broadcast_to(peak, (TILE, TILE))
        peaks[here, :] = peak
        ones = jnp.ones((TILE, hd), jnp.bfloat16)
        total = None
        for j in range(0, slots, 2):
            values = jnp.concatenate(
                [
                    jnp.concatenate([cbuf[lists[h, j + k, tile], :, hd:], ones], axis=1)
                    for k in range(2)
                ],
                axis=0,
            )
            weights = jnp.concatenate(
                [
                    jnp.exp2(
                        (scores[here, (j + k) * TILE : (j + k + 1) * TILE] - peak) * scale
                    ).astype(jnp.bfloat16)
                    for k in range(2)
                ],
                axis=1,
            )
            mixed = jnp.dot(weights, values, preferred_element_type=jnp.float32)
            total = mixed if total is None else total + mixed
        accum[here, :] = total
        return 0

    lax.fori_loop(0, GROUP, cache_mix, 0, unroll=True)

    def span_mix(kb, _):
        col = pl.multiple_of(span_at + (kb - first) * rows, rows)
        ones = jnp.ones((rows, hd), jnp.bfloat16)
        values = kvbuf[pl.ds(kb * 2, 2), :, :, hd:].reshape(rows, hd)
        values = jnp.concatenate([values, ones], axis=1)
        for t in range(GROUP):
            here = slice(t * TILE, (t + 1) * TILE)
            peak = peaks[here, :]
            weights = jnp.concatenate(
                [
                    jnp.exp2(
                        (scores[here, pl.ds(col + u * TILE, TILE)] - peak) * scale
                    ).astype(jnp.bfloat16)
                    for u in range(GROUP)
                ],
                axis=1,
            )
            accum[here, :] += jnp.dot(weights, values, preferred_element_type=jnp.float32)
        return 0

    lax.fori_loop(first, b + 1 if stats is None else half // GROUP, span_mix, 0)
    if stats is not None:
        for t in range(GROUP):
            here = slice(t * TILE, (t + 1) * TILE)
            level_of = peaks[here, :] * scale + jnp.log(accum[here, hd:]) * math.log2(math.e)
            stats[h, b * GROUP + t - half] = jnp.transpose(level_of)[:1, :]
    obuf[h, pl.ds(base, rows), :] = (accum[:, :hd] / accum[:, hd:]).astype(jnp.bfloat16)


def attend_local(i, pos, me, tiles, qloc, kvloc, mask, scores, peaks, accum, o_near, l_near):
    hd = o_near.shape[-1]
    scale = math.log2(math.e) / math.sqrt(hd)
    at = pl.multiple_of(i // 2 * 2 * hd, 2 * hd)
    q = jnp.concatenate(
        [qloc[:, pl.ds(pl.multiple_of((i * GROUP + k) * hd, hd), hd)] for k in range(GROUP)], axis=0
    )
    peaks[...] = jnp.full(peaks.shape, NEG, jnp.float32)

    def score(u, diagonal):
        s = dot_t(q, kvloc[u // 2, u % 2, :, pl.ds(at, hd)])
        s = keep_if(mask[me, tiles // 2 + u], 0, s)
        if diagonal:
            lower = lax.broadcasted_iota(jnp.int32, (TILE, TILE), 1) <= lax.broadcasted_iota(
                jnp.int32, (TILE, TILE), 0
            )
            s = jnp.concatenate(
                [jnp.where(lower, s[k * TILE : (k + 1) * TILE], NEG) for k in range(GROUP)], axis=0
            )
        scores[:, pl.ds(pl.multiple_of(u * TILE, TILE), TILE)] = s
        peaks[...] = jnp.maximum(peaks[...], s)

    def earlier(u, _):
        score(u, False)
        return 0

    lax.fori_loop(0, pos, earlier, 0)
    score(pos, True)
    peak = jnp.max(peaks[...], axis=1, keepdims=True)
    peaks[...] = jnp.broadcast_to(peak, peaks.shape)
    accum[...] = jnp.zeros(accum.shape, jnp.float32)

    def mix(u, _):
        values = jnp.concatenate(
            [
                kvloc[u // 2, u % 2, :, pl.ds(pl.multiple_of(at + hd, hd), hd)],
                jnp.ones((TILE, hd), jnp.bfloat16),
            ],
            axis=1,
        )
        weights = jnp.exp2(
            (scores[:, pl.ds(pl.multiple_of(u * TILE, TILE), TILE)] - peaks[...]) * scale
        ).astype(jnp.bfloat16)
        accum[...] += jnp.dot(weights, values, preferred_element_type=jnp.float32)
        return 0

    lax.fori_loop(0, pos + 1, mix, 0)
    for k in range(GROUP):
        here = slice(k * TILE, (k + 1) * TILE)
        total = accum[here, hd:]
        o_near[i * GROUP + k] = accum[here, :hd] / total
        l_near[i * GROUP + k] = peaks[here, :] * scale + jnp.log(total) * math.log2(math.e)


def fused(
    n, kv_heads, slots,
    lists_ref, counts_ref, mask_ref, q_ref, kv_ref, c_ref, out_ref,
    lists, counts, mask, qbuf, kvbuf, cbuf, obuf, scores, peaks, accum,
    above_sem, below_sem, s_sem, c_sem, l_sem, kv_send, kv_recv, f_send, f_recv, q_send, q_recv, o_send, o_recv,
):
    me = lax.axis_index("seq")
    heads, _, hd = qbuf.shape
    chips = n // 2
    core = lax.rem(me, 2)
    sibling = me + 1 - 2 * core
    my_chip = me // 2

    blocks = n // GROUP
    half = blocks // 2

    def far_first(step):
        z = me // GROUP
        upper = z // half
        across = 1 - step // half
        far = lax.rem(step, half)
        near = lax.rem(z + 1 + step, half)
        low = jnp.where(across == 1, far, near)
        high = near
        target = lax.rem(upper + across, 2)
        return target * half + jnp.where(target == 0, low, high)

    levels = n // GROUP
    level = me // GROUP
    pos = lax.rem(me, GROUP)
    has_above = level + 1 < levels
    has_below = level > 0
    barrier = pltpu.get_barrier_semaphore()

    def tell(sem, device):
        pl.semaphore_signal(sem, inc=1, device_id={"seq": device}, device_id_type=MESH)

    for k in range(1, GROUP):
        tell(barrier, level * GROUP + lax.rem(pos + k, GROUP))

    @pl.when(has_above)
    def _():
        tell(barrier, me + GROUP)

    @pl.when(has_below)
    def _():
        tell(barrier, me - GROUP)

    cache_copy = pltpu.make_async_copy(c_ref, cbuf, c_sem)
    cache_copy.start()

    small = [
        pltpu.make_async_copy(src, dst, s_sem.at[k])
        for k, (src, dst) in enumerate(((lists_ref, lists), (counts_ref, counts), (mask_ref, mask)))
    ]
    for copy in small:
        copy.start()
    def own_q(h):
        return pltpu.make_async_copy(
            q_ref.at[:, pl.ds(pl.multiple_of((me * heads + h) * hd, hd), hd)],
            qbuf.at[h, pl.ds(pl.multiple_of(me * TILE, TILE), TILE), :],
            l_sem.at[h],
        )

    def kv_cols(chip):
        return pl.ds(pl.multiple_of((2 * chip * kv_heads // n) * 2 * hd, 2 * hd), 2 * hd)

    own_kv = pltpu.make_async_copy(kv_ref.at[:, kv_cols(my_chip)], kvbuf.at[my_chip, core], l_sem.at[heads])
    own_kv.start()
    for h in range(heads):
        own_q(h).start()
    pl.semaphore_wait(barrier, GROUP - 1 + has_above.astype(jnp.int32) + has_below.astype(jnp.int32))

    def q_to(peer, h):
        pltpu.make_async_remote_copy(
            src_ref=q_ref.at[:, pl.ds(pl.multiple_of((peer * heads + h) * hd, hd), hd)],
            dst_ref=qbuf.at[h, pl.ds(pl.multiple_of(me * TILE, TILE), TILE), :],
            send_sem=q_send,
            recv_sem=q_recv.at[h],
            device_id={"seq": peer},
            device_id_type=MESH,
        ).start()

    def send_kv(chip):
        pltpu.make_async_remote_copy(
            src_ref=kv_ref.at[:, kv_cols(chip)],
            dst_ref=kvbuf.at[my_chip, core],
            send_sem=kv_send,
            recv_sem=kv_recv,
            device_id={"seq": 2 * chip + core},
            device_id_type=MESH,
        ).start()

    pairs = GROUP // 2

    def kv_to_level(at, first):
        for k in range(first, pairs):
            send_kv(at * pairs + lax.rem(pos // 2 + k, pairs))

    @pl.when(has_above)
    def _():
        tell(below_sem, me + GROUP)
        send_kv(my_chip + pairs)
        for h in range(heads):
            q_to(me + GROUP, h)

    @pl.when(has_below)
    def _():
        tell(above_sem, me - GROUP)
        send_kv(my_chip - pairs)
        for h in range(heads):
            q_to(me - GROUP, h)

    def learn(k, first):
        @pl.when(level + k < levels)
        def _():
            pl.semaphore_wait(above_sem, 1)

            @pl.when(has_below)
            def _():
                tell(above_sem, me - GROUP)

            kv_to_level(level + k, first)

        @pl.when(level >= k)
        def _():
            pl.semaphore_wait(below_sem, 1)

            @pl.when(has_above)
            def _():
                tell(below_sem, me + GROUP)

            kv_to_level(level - k, first)

        return 0

    learn(1, 1)
    lax.fori_loop(2, levels, lambda k, _: learn(k, 0), 0)
    kv_to_level(level, 1)

    def send_q(step, _):
        h = step // n
        turn = lax.rem(step, n)
        peer = far_first(turn // GROUP) * GROUP + lax.rem(me + turn, GROUP)

        @pl.when((peer != me) & (peer != me + GROUP) & (peer != me - GROUP))
        def _():
            q_to(peer, h)

        return 0

    lax.fori_loop(0, heads * n, send_q, 0)

    def take(ref, sem):
        pltpu.make_async_copy(ref, ref, sem).wait()

    own_kv.wait()
    take(kvbuf.at[pl.ds(0, chips - 1), 0], kv_recv)
    forward = pltpu.make_async_remote_copy(
        src_ref=kvbuf.at[:, core],
        dst_ref=kvbuf.at[:, core],
        send_sem=f_send,
        recv_sem=f_recv,
        device_id={"seq": sibling},
        device_id_type=MESH,
    )
    forward.start()
    cache_copy.wait()
    for copy in small:
        copy.wait()
    forward.wait()

    def one_head(h, _):
        own_q(h).wait()
        take(qbuf.at[h, pl.ds(0, (n - 1) * TILE), :], q_recv.at[h])

        def one_block(step, _):
            b = far_first(step)
            attend_block(
                h, b, slots, qbuf, kvbuf, cbuf, lists, counts, mask, scores, peaks, accum, obuf
            )
            cols = pl.ds(pl.multiple_of((me * heads + h) * hd, hd), hd)
            for t in range(GROUP):
                peer = b * GROUP + t
                src = obuf.at[h, pl.ds(pl.multiple_of(peer * TILE, TILE), TILE), :]

                @pl.when(peer != me)
                def _():
                    pltpu.make_async_remote_copy(
                        src_ref=src,
                        dst_ref=out_ref.at[:, cols],
                        send_sem=o_send,
                        recv_sem=o_recv,
                        device_id={"seq": peer},
                        device_id_type=MESH,
                    ).start()

                @pl.when(peer == me)
                def _():
                    pltpu.make_async_copy(src, out_ref.at[:, cols], l_sem.at[heads + 1]).start()

            return 0

        lax.fori_loop(0, blocks, one_block, 0)
        return 0

    lax.fori_loop(0, heads, one_head, 0)

    wide = pl.ds(0, (n - 1) * heads * hd)
    take(kvbuf.at[pl.ds(0, chips - 1), 0], kv_send)
    take(q_ref.at[:, wide], q_send)
    take(q_ref.at[:, wide], o_send)
    take(out_ref.at[:, wide], o_recv)
    take(out_ref.at[:, pl.ds(0, heads * hd)], l_sem.at[heads + 1])


def fused_split(
    n, kv_heads, slots,
    lists_ref, counts_ref, mask_ref, q_ref, kv_ref, c_ref, out_ref,
    lists, counts, mask, qbuf, kvbuf, cbuf, obuf, scores, peaks, accum,
    qloc, kvloc, o_near, l_near, stats, far_stats, far_o,
    above_sem, below_sem, s_sem, c_sem, l_sem, kv_send, kv_recv, f_send, f_recv, q_send, q_recv, o_send, o_recv,
    loc_send, loc_recv, lf_send, lf_recv, p_sem, ul_recv, st_send, st_recv, m_sem,
):
    me = lax.axis_index("seq")
    heads, _, hd = qbuf.shape
    chips = n // 2
    core = lax.rem(me, 2)
    sibling = me + 1 - 2 * core
    my_chip = me // 2

    blocks = n // GROUP
    half = blocks // 2

    def far_first(step, h):
        z = me // GROUP
        upper = z // half
        across = 1 - step // half
        far = lax.rem(step, half)
        near = lax.rem(z + 1 + step, half)
        low = jnp.where((across == 1) & (h >= 0), far, near)
        high = jnp.where((across == 1) & (h == heads - 1), half - 1 - far, near)
        target = lax.rem(upper + across, 2)
        return target * half + jnp.where(target == 0, low, high)

    levels = n // GROUP
    level = me // GROUP
    pos = lax.rem(me, GROUP)
    has_above = level + 1 < levels
    has_below = level > 0
    barrier = pltpu.get_barrier_semaphore()

    def tell(sem, device):
        pl.semaphore_signal(sem, inc=1, device_id={"seq": device}, device_id_type=MESH)

    for k in range(1, GROUP):
        tell(barrier, level * GROUP + lax.rem(pos + k, GROUP))

    @pl.when(has_above)
    def _():
        tell(barrier, me + GROUP)

    @pl.when(has_below)
    def _():
        tell(barrier, me - GROUP)

    cache_copy = pltpu.make_async_copy(c_ref, cbuf, c_sem)
    cache_copy.start()

    small = [
        pltpu.make_async_copy(src, dst, s_sem.at[k])
        for k, (src, dst) in enumerate(((lists_ref, lists), (counts_ref, counts), (mask_ref, mask)))
    ]
    for copy in small:
        copy.start()
    def own_q(h):
        return pltpu.make_async_copy(
            q_ref.at[:, pl.ds(pl.multiple_of((me * heads + h) * hd, hd), hd)],
            qbuf.at[h, pl.ds(pl.multiple_of(me * TILE, TILE), TILE), :],
            l_sem.at[h],
        )

    def kv_cols(chip):
        return pl.ds(pl.multiple_of((2 * chip * kv_heads // n) * 2 * hd, 2 * hd), 2 * hd)

    own_kv = pltpu.make_async_copy(kv_ref.at[:, kv_cols(my_chip)], kvbuf.at[my_chip, core], l_sem.at[heads])
    own_kv.start()
    near_n = n // 2
    near_chips = chips // 2
    low = me < near_n
    high = me >= near_n
    is_cut = my_chip == 0
    loc_kv = kv_ref.at[:, pl.ds(0, 2 * hd)]
    loc_slot = lax.rem(my_chip, near_chips)
    own_loc_q = pltpu.make_async_copy(q_ref.at[:, pl.ds(0, 2 * heads * hd)], qloc, p_sem.at[0])
    own_loc_kv = pltpu.make_async_copy(loc_kv, kvloc.at[loc_slot, core], p_sem.at[1])

    @pl.when(high)
    def _():
        own_loc_q.start()
        own_loc_kv.start()

    for h in range(heads):
        own_q(h).start()
    pl.semaphore_wait(barrier, GROUP - 1 + has_above.astype(jnp.int32) + has_below.astype(jnp.int32))

    def q_to(peer, h):
        pltpu.make_async_remote_copy(
            src_ref=q_ref.at[:, pl.ds(pl.multiple_of((peer * heads + h) * hd, hd), hd)],
            dst_ref=qbuf.at[h, pl.ds(pl.multiple_of(me * TILE, TILE), TILE), :],
            send_sem=q_send,
            recv_sem=q_recv.at[h],
            device_id={"seq": peer},
            device_id_type=MESH,
        ).start()

    def send_kv(chip):
        @pl.when(low | (chip > 0))
        def _():
            pltpu.make_async_remote_copy(
                src_ref=kv_ref.at[:, kv_cols(chip)],
                dst_ref=kvbuf.at[my_chip, core],
                send_sem=kv_send,
                recv_sem=kv_recv,
                device_id={"seq": 2 * chip + core},
                device_id_type=MESH,
            ).start()

    pairs = GROUP // 2

    def kv_to_level(at, first):
        for k in range(first, pairs):
            send_kv(at * pairs + lax.rem(pos // 2 + k, pairs))

    @pl.when(has_above)
    def _():
        tell(below_sem, me + GROUP)
        send_kv(my_chip + pairs)
        for h in range(heads):
            q_to(me + GROUP, h)

    @pl.when(has_below)
    def _():
        tell(above_sem, me - GROUP)
        send_kv(my_chip - pairs)
        for h in range(heads):
            q_to(me - GROUP, h)

    def learn(k, first):
        @pl.when(level + k < levels)
        def _():
            pl.semaphore_wait(above_sem, 1)

            @pl.when(has_below)
            def _():
                tell(above_sem, me - GROUP)

            kv_to_level(level + k, first)

        @pl.when(level >= k)
        def _():
            pl.semaphore_wait(below_sem, 1)

            @pl.when(has_above)
            def _():
                tell(below_sem, me + GROUP)

            kv_to_level(level - k, first)

        return 0

    learn(1, 1)
    lax.fori_loop(2, levels, lambda k, _: learn(k, 0), 0)
    kv_to_level(level, 1)

    def send_q(step, _):
        h = step // n
        turn = lax.rem(step, n)
        peer = far_first(turn // GROUP, h) * GROUP + lax.rem(me + turn, GROUP)

        @pl.when((peer != me) & (peer != me + GROUP) & (peer != me - GROUP))
        def _():
            q_to(peer, h)

        return 0

    @pl.when(high)
    def _():
        for k in range(1, near_chips):
            pltpu.make_async_remote_copy(
                src_ref=loc_kv,
                dst_ref=kvloc.at[loc_slot, core],
                send_sem=loc_send,
                recv_sem=loc_recv,
                device_id={"seq": 2 * (near_chips + lax.rem(my_chip + k, near_chips)) + core},
                device_id_type=MESH,
            ).start()

    lax.fori_loop(0, heads * n, send_q, 0)

    def take(ref, sem):
        pltpu.make_async_copy(ref, ref, sem).wait()

    def to_sibling(ref, send, recv):
        return pltpu.make_async_remote_copy(
            src_ref=ref,
            dst_ref=ref,
            send_sem=send,
            recv_sem=recv,
            device_id={"seq": sibling},
            device_id_type=MESH,
        )

    own_kv.wait()
    cache_copy.wait()
    for copy in small:
        copy.wait()
    forward_all = to_sibling(kvbuf.at[:, core], f_send, f_recv)
    forward_low = to_sibling(kvbuf.at[pl.ds(0, near_chips), core], f_send, f_recv)
    forward_loc = to_sibling(kvloc.at[:, core], lf_send, lf_recv)

    @pl.when(is_cut)
    def _():
        take(kvbuf.at[pl.ds(0, near_chips - 1), 0], kv_recv)
        forward_low.start()
        forward_low.wait()

    @pl.when(jnp.logical_not(is_cut))
    def _():
        take(kvbuf.at[pl.ds(0, chips - 1), 0], kv_recv)
        forward_all.start()
        forward_all.wait()

    @pl.when(high)
    def _():
        own_loc_q.wait()
        own_loc_kv.wait()
        take(kvloc.at[pl.ds(0, near_chips - 1), 0], loc_recv)
        forward_loc.start()

    def local(i, _):
        attend_local(i, me - near_n, me, n, qloc, kvloc, mask, scores, peaks, accum, o_near, l_near)
        return 0

    def one_head(h, _):
        @pl.when(high & (h == 1))
        def _():
            forward_loc.wait()
            lax.fori_loop(0, 2, local, 0)

        own_q(h).wait()
        take(qbuf.at[h, pl.ds(0, (n - 1) * TILE), :], q_recv.at[h])

        def one_block(step, _):
            b = far_first(step, h)
            partial = is_cut & (b >= half)

            @pl.when(partial)
            def _():
                attend_block(
                    h, b, slots, qbuf, kvbuf, cbuf, lists, counts, mask, scores, peaks, accum, obuf,
                    stats, near_n,
                )
                for t in range(GROUP):
                    peer = b * GROUP + t
                    for src, dst, send, recv in (
                        (obuf.at[h, pl.ds(pl.multiple_of(peer * TILE, TILE), TILE), :], far_o.at[h, core], o_send, ul_recv),
                        (stats.at[h, peer - near_n], far_stats.at[h, core], st_send, st_recv),
                    ):
                        pltpu.make_async_remote_copy(
                            src_ref=src,
                            dst_ref=dst,
                            send_sem=send,
                            recv_sem=recv.at[h],
                            device_id={"seq": peer},
                            device_id_type=MESH,
                        ).start()

            @pl.when(jnp.logical_not(partial))
            def _():
                attend_block(
                    h, b, slots, qbuf, kvbuf, cbuf, lists, counts, mask, scores, peaks, accum, obuf
                )
                cols = pl.ds(pl.multiple_of((me * heads + h) * hd, hd), hd)
                for t in range(GROUP):
                    peer = b * GROUP + t
                    src = obuf.at[h, pl.ds(pl.multiple_of(peer * TILE, TILE), TILE), :]

                    @pl.when(peer != me)
                    def _():
                        pltpu.make_async_remote_copy(
                            src_ref=src,
                            dst_ref=out_ref.at[:, cols],
                            send_sem=o_send,
                            recv_sem=o_recv,
                            device_id={"seq": peer},
                            device_id_type=MESH,
                        ).start()

                    @pl.when(peer == me)
                    def _():
                        pltpu.make_async_copy(src, out_ref.at[:, cols], l_sem.at[heads + 1]).start()

            return 0

        lax.fori_loop(0, blocks, one_block, 0)
        return 0

    lax.fori_loop(0, heads, one_head, 0)

    def tile_cols(count):
        return q_ref.at[:, pl.ds(0, count * hd)]

    @pl.when(high)
    def _():
        def merge_head(h, _):
            take(far_o.at[h], ul_recv.at[h])
            take(far_stats.at[h], st_recv.at[h])

            def merge(owner, _):
                i = owner * heads + h
                cols = pl.ds(pl.multiple_of(i * hd, hd), hd)
                l_far = jnp.transpose(jnp.broadcast_to(far_stats[h, owner], (TILE, TILE)))
                l_own = l_near[i]
                top = jnp.maximum(l_far, l_own)
                w_far = jnp.exp2(l_far - top)
                w_own = jnp.exp2(l_own - top)
                mixed = far_o[h, owner].astype(jnp.float32) * w_far + o_near[i] * w_own
                far_o[h, owner] = (mixed / (w_far + w_own)).astype(jnp.bfloat16)
                pltpu.make_async_copy(far_o.at[h, owner], out_ref.at[:, cols], m_sem).start()
                return 0

            lax.fori_loop(0, 2, merge, 0)
            return 0

        lax.fori_loop(0, heads, merge_head, 0)
        take(kvbuf.at[pl.ds(0, chips - 2), 0], kv_send)
        take(kvloc.at[pl.ds(0, near_chips - 1), 0], loc_send)
        take(tile_cols((n - 3) * heads), o_recv)
        take(far_o, m_sem)

    @pl.when(low)
    def _():
        take(kvbuf.at[pl.ds(0, chips - 1), 0], kv_send)
        take(tile_cols((n - 1) * heads), o_recv)

    @pl.when(is_cut)
    def _():
        take(stats, st_send)

    take(tile_cols((n - 1) * heads), q_send)
    take(tile_cols((n - 1) * heads), o_send)
    take(out_ref.at[:, pl.ds(0, heads * hd)], l_sem.at[heads + 1])


def per_device(queries, new_kv, cache, tile_lists, tile_counts, tile_mask):
    n = lax.axis_size("seq")
    hd = cache.shape[2] // 2
    kv_heads = new_kv.shape[1] // (2 * hd)
    heads, tiles, slots = tile_lists.shape
    tokens = tiles * TILE
    rows = GROUP * TILE
    reach = min(REACH + 1, tiles // GROUP)
    bf, f32 = jnp.bfloat16, jnp.float32
    dma = pltpu.SemaphoreType.DMA
    hbm = pl.BlockSpec(memory_space=pl.ANY)
    lists_of = tile_lists.transpose(0, 2, 1)
    levels = n // GROUP
    operands = lists_of, tile_counts, tile_mask, queries, new_kv, cache.reshape(-1, TILE, 2 * hd)
    if levels % 2 == 0 and levels <= REACH + 1 and 2 * kv_heads == n and heads == GROUP and n == tiles:
        near = n // 2
        vm, sm = pltpu.VMEM, pltpu.SMEM
        return pl.pallas_call(
            functools.partial(fused_split, n, kv_heads, slots),
            out_shape=vm(queries.shape, bf),
            in_specs=[hbm] * 6,
            out_specs=hbm,
            scratch_shapes=[
                sm((heads, slots, tiles), jnp.int32),
                sm((heads, tiles), jnp.int32),
                sm(tile_mask.shape, jnp.int32),
                vm((heads, tokens, hd), bf),
                vm((n // 2, 2, TILE, 2 * hd), bf),
                vm((cache.shape[1] // TILE, TILE, 2 * hd), bf),
                vm((heads, tokens, hd), bf),
                vm((rows, slots * TILE + reach * rows), f32),
                vm((rows, TILE), f32),
                vm((rows, 2 * hd), f32),
                vm((TILE, 2 * heads * hd), bf),
                vm((near // 2, 2, TILE, 2 * hd), bf),
                vm((2 * heads, TILE, hd), f32),
                vm((2 * heads, TILE, hd), f32),
                vm((heads, near, 1, TILE), f32),
                vm((heads, 2, 1, TILE), f32),
                vm((heads, 2, TILE, hd), bf),
                pltpu.SemaphoreType.REGULAR, pltpu.SemaphoreType.REGULAR,
                dma((3,)), dma, dma((heads + 2,)), dma, dma, dma, dma, dma, dma((heads,)), dma, dma,
                dma, dma, dma, dma, dma((2,)), dma((heads,)), dma, dma((heads,)), dma,
            ],
            compiler_params=pltpu.CompilerParams(
                collective_id=0, has_side_effects=True, vmem_limit_bytes=60 * 1024 * 1024
            ),
        )(*operands)
    return pl.pallas_call(
        functools.partial(fused, n, kv_heads, slots),
        out_shape=pltpu.VMEM(queries.shape, bf),
        in_specs=[hbm] * 6,
        out_specs=hbm,
        scratch_shapes=[
            pltpu.SMEM((heads, slots, tiles), jnp.int32),
            pltpu.SMEM((heads, tiles), jnp.int32),
            pltpu.SMEM(tile_mask.shape, jnp.int32),
            pltpu.VMEM((heads, tokens, hd), bf),
            pltpu.VMEM((n // 2, 2, TILE, 2 * hd), bf),
            pltpu.VMEM((cache.shape[1] // TILE, TILE, 2 * hd), bf),
            pltpu.VMEM((heads, tokens, hd), bf),
            pltpu.VMEM((rows, slots * TILE + reach * rows), f32),
            pltpu.VMEM((rows, TILE), f32),
            pltpu.VMEM((rows, 2 * hd), f32),
            pltpu.SemaphoreType.REGULAR, pltpu.SemaphoreType.REGULAR,
            dma((3,)), dma, dma((heads + 2,)), dma, dma, dma, dma, dma, dma((heads,)), dma, dma,
        ],
        compiler_params=pltpu.CompilerParams(
            collective_id=0, has_side_effects=True, vmem_limit_bytes=60 * 1024 * 1024
        ),
    )(*operands)


def solution(mesh):
    placed = (
        P(("grp", "seq"), None),
        P(("grp", "seq"), None),
        P(("grp", "seq"), None, None),
        P(("grp", "seq"), None, None),
        P(("grp", "seq"), None),
        P("grp", None),
    )
    return jax.shard_map(
        per_device, mesh=mesh, in_specs=placed, out_specs=P(("grp", "seq"), None), check_vma=False
    )
```
